32 devices in a mesh: grp: 2 (over x), ep: 16 (over z, y, core).
Axes of the slice: x: 2, y: 2, z: 4, core: 2. Of those that a mesh axis runs over, the one named last changes fastest.
Arguments:
- tokens: bfloat16 [1024, 4096], P('ep'), may hold values from -6 to 6
- norm_gain: float32 [4096], replicated, may hold values from 0.1 to 1.9
- expert_ids: int32 [1024, 8], P('ep'), may hold values from 0 to 15, all different within a row; in each aligned block of 64 rows (0 to 63, 64 to 127, ...) at most 64 rows name the same one
- gate_scores: float32 [1024, 8], P('ep'), may hold values from 0.05 to 1
- w_gate: bfloat16 [16, 1536, 4096], P('ep', 'grp'), may hold values from -0.09375 to 0.09375
- w_up: bfloat16 [16, 1536, 4096], P('ep', 'grp'), may hold values from -0.09375 to 0.09375
- w_down: bfloat16 [16, 1536, 4096], P('ep', 'grp'), may hold values from -0.21875 to 0.21875
Outputs:
- moe_out: bfloat16 [1024, 4096], P('ep', 'grp')
The draws below stay inside these ranges and needn't reach their ends.
Inputs may be any that keep to these rules, and one draw needn't show every extreme that they name: `expert_ids`: each row names 8 different experts. Within each aligned block of 64 rows (the rows of one device) no expert is named by more than 64 rows, and this bound is reached.
All inputs are finite; a program needn't handle non-finite values.
Results may differ from the reference program's by a relative error of at most 0.009.
Values may be sent and summed in bfloat16 or wider, within the bound.
A program may use at most 128 MiB of HBM per device.

```python
import math
import jax
import jax.numpy as jnp
import numpy as np
from jax import lax

D = 4096
H = 1536
TOPK = 8
TOK_DEV = 64
E = 16
TOKENS = 1024
CAP = 64
N_GRP = 2
N_EP = 16


def strengthened(result, rng, source, target, shards_of, factor):
    owner, partner = [(jnp.arange(result.shape[position]) // (result.shape[position] // shards_of)).reshape([-1 if axis == position else 1 for axis in range(result.ndim)]) for position in (source, target)]
    chosen = jax.random.permutation(rng, shards_of)[partner]
    strong = (owner == chosen) | (owner == (partner + shards_of // 2) % shards_of)
    return jnp.where(strong, factor * result, result)


def block_scale(rng, shape, split, smallest, top_value):
    def one(axis_at, shards_of):
        steps = jax.random.uniform(jax.random.fold_in(jax.random.fold_in(rng, 6), axis_at), (shards_of,), jnp.float32, smallest / len(split), top_value / len(split))
        return jnp.repeat(jnp.exp(steps), shape[axis_at] // shards_of).reshape((-1,) + (1,) * (len(shape) - axis_at - 1))

    gain = one(*split[0])
    for cut in split[1:]:
        gain = gain * one(*cut)
    return gain


def deal_out(own_key, own, number, rows, count, top, reach, slope):
    sequence = jax.random.permutation(own_key, count)
    heavy_load, usual = shares(count, rows * top, reach, slope, True), shares(count, rows * top, reach, slope, False)
    places = jnp.arange(count)

    def named(lengths, rotation):
        used = int((lengths > 0).sum())
        fixed = max(1, used // 4)
        passed = fixed + (places - fixed + rotation * (used - fixed)) % max(1, count - fixed)
        return jnp.zeros((count,), jnp.int32).at[sequence[jnp.where(places < fixed, places, passed)]].set(jnp.asarray(lengths, jnp.int32))

    lengths = jnp.where(number % 4 == 0, named(heavy_load, number // 4), named(usual, number - number // 4 - 1))
    mixed = jax.random.permutation(jax.random.fold_in(own, 3), count)
    source_of, receiver = mixed[0:count // 2 * 2:2], mixed[1:count // 2 * 2:2]
    margin = jnp.minimum(lengths[source_of] - 1, reach - lengths[receiver]) // 2
    margin = jnp.where((source_of == sequence[0]) | (receiver == sequence[0]) | (lengths[receiver] == 0), 0, jnp.maximum(margin, 0))
    passed = jax.random.randint(jax.random.fold_in(own, 4), (count // 2,), 0, 1 << 20) % (margin + 1)
    lengths = lengths.at[source_of].add(-passed).at[receiver].add(passed)
    items = jnp.searchsorted(jnp.cumsum(lengths), jnp.arange(rows * top), side="right").astype(jnp.int32)
    listing = items.reshape(top, rows).T
    listing = listing[jax.random.permutation(jax.random.fold_in(own, 1), rows)]
    rotation = jax.random.randint(jax.random.fold_in(own, 2), (rows, 1), 0, top)
    return jnp.take_along_axis(listing, (jnp.arange(top)[None, :] + rotation) % top, axis=1)


def shares(amount, total, most, slope, full):
    weights = [(1 << 20) // math.isqrt(standing ** slope) + 1 for standing in range(1, amount + 1)]
    largest = most if full else min(most, max(-(-total // amount), total * weights[0] // sum(weights)))
    least = 1 if total - largest >= amount - 1 else 0
    holding, spare = [largest] + [least] * (amount - 1), total - largest - least * (amount - 1)
    while spare > 0:
        free = [i for i in range(1, amount) if holding[i] < largest] or [i for i in range(1, amount) if holding[i] < most]
        mass, remaining = sum([weights[i] for i in free]), spare
        for i in free:
            extra = min(most - holding[i], max(1, remaining * weights[i] // mass), spare)
            holding[i] = holding[i] + extra
            spare = spare - extra
    return np.array(holding)


def scatter_about(own_key, shape, spread, limit, split=(), held_as=jnp.bfloat16):
    entries = spread * jax.random.normal(own_key, shape, jnp.float32)
    if split:
        entries = entries * block_scale(own_key, shape, split, -0.22, 0.18)
    return jnp.clip(entries, -limit, limit).astype(held_as)


def heavy_noise(stream_key, shape, spread, reach, cuts, heavy, kind=jnp.bfloat16):
    result = spread * jax.random.normal(stream_key, shape, jnp.float32)
    if cuts:
        result = result * block_scale(stream_key, shape, cuts, -0.22, 0.18)
    return jnp.clip(strengthened(result, jax.random.fold_in(stream_key, 3), *heavy), -reach, reach).astype(kind)


def setup_inputs(seed: int = 0) -> dict:
    key_of = jax.random.split(jax.random.key(seed), 8)
    tokens = scatter_about(key_of[0], (TOKENS, D), 1.0, 6.0, ((0, 16),))
    norm_gain = jnp.clip(1.0 + 0.18 * jax.random.normal(key_of[1], (D,), jnp.float32), 0.1, 1.9)
    expert_ids_keys = jax.random.split(jax.random.fold_in(key_of[2], 1), TOKENS // TOK_DEV)
    expert_ids_turns = jax.random.permutation(jax.random.fold_in(key_of[2], 3), TOKENS // TOK_DEV)
    expert_ids = jax.vmap(lambda own, number: deal_out(jax.random.fold_in(key_of[2], 2), own, number, TOK_DEV, E, TOPK, CAP, 2))(expert_ids_keys, expert_ids_turns).reshape((TOKENS, TOPK))
    gate_scores = jnp.clip(jnp.exp(math.log(1.0) - 2.9957323 * jax.random.uniform(key_of[3], (TOKENS, TOPK), jnp.float32) ** block_scale(key_of[3], (TOKENS, TOPK), ((0, 16),), -0.2, 0.2)), 0.05, 1.0)
    w_gate = scatter_about(key_of[4], (E, H, D), D ** -0.5, 0.09375, ((0, 16), (1, 2)))
    w_up = scatter_about(key_of[5], (E, H, D), D ** -0.5, 0.09375, ((0, 16), (1, 2)))
    w_down = heavy_noise(key_of[6], (E, H, D), H ** -0.5, 0.21875, ((0, 16), (1, 2)), (1, 2, 2, 2.0))
    return {"tokens": tokens, "norm_gain": norm_gain, "expert_ids": expert_ids, "gate_scores": gate_scores, "w_gate": w_gate, "w_up": w_up, "w_down": w_down}


def reference(tokens, norm_gain, expert_ids, gate_scores, w_gate, w_up, w_down):
    floated = tokens.astype(jnp.float32)
    scaled = lax.rsqrt(lax.optimization_barrier(jnp.mean(floated * floated, axis=1, keepdims=True)) + 1e-06)
    normed = (floated * scaled * norm_gain[None, :]).astype(jnp.bfloat16)
    mixing = (gate_scores / lax.optimization_barrier(jnp.sum(gate_scores, axis=1, keepdims=True))).reshape(-1)
    flat_ids = expert_ids.reshape(-1)
    bucket_rows = N_EP * CAP
    block_width = H // N_GRP
    limits = jnp.arange(bucket_rows, dtype=jnp.int32)

    def one_expert(running, expert):
        matches = flat_ids == expert
        found_slots = jnp.nonzero(matches, size=bucket_rows, fill_value=0)[0].astype(jnp.int32)
        number = jnp.sum(matches.astype(jnp.int32))
        token_rows = (found_slots // TOPK).astype(jnp.int32)
        chosen = normed[token_rows]
        gate_proj = jnp.dot(chosen, w_gate[expert].T, preferred_element_type=jnp.float32)
        up_proj = jnp.dot(chosen, w_up[expert].T, preferred_element_type=jnp.float32)
        hidden = (jax.nn.silu(gate_proj) * up_proj).astype(jnp.bfloat16)
        down_rows = w_down[expert]
        gathered = jnp.zeros((bucket_rows, D), jnp.float32)
        for slice_index in range(N_GRP):
            lower = slice_index * block_width
            block_part = jnp.dot(hidden[:, lower:lower + block_width], down_rows[lower:lower + block_width], preferred_element_type=jnp.float32).astype(jnp.bfloat16)
            gathered = gathered + lax.optimization_barrier(block_part).astype(jnp.float32)
        weights = jnp.where(limits < number, mixing[found_slots], jnp.zeros_like(mixing[found_slots]))
        running = running.at[token_rows].add(weights[:, None] * gathered)
        return (running, None)
    running, _ = lax.scan(one_expert, jnp.zeros((TOKENS, D), jnp.float32), jnp.arange(E, dtype=jnp.int32))
    return running.astype(jnp.bfloat16)
```

```python
import functools

import jax
import jax.numpy as jnp
from jax import lax
from jax.experimental import pallas as pl
from jax.experimental.pallas import tpu as pltpu
from jax.sharding import PartitionSpec as P


def finish_expert(gate_proj, up_proj, w_down, sources, item_count, model_width):
    hidden = (jax.nn.silu(gate_proj) * up_proj).astype(jnp.bfloat16)
    outputs = jnp.dot(hidden, w_down[0], preferred_element_type=jnp.float32).astype(jnp.bfloat16)
    return outputs.reshape(sources, item_count, model_width)


def expert_block(received, w_gate, w_up, w_down):
    sources, item_count, model_width = received.shape
    flat_rows = received.reshape(sources * item_count, model_width)
    contract = (((1,), (1,)), ((), ()))
    gate_proj = lax.dot_general(flat_rows, w_gate[0], contract, preferred_element_type=jnp.float32)
    up_proj = lax.dot_general(flat_rows, w_up[0], contract, preferred_element_type=jnp.float32)
    return finish_expert(gate_proj, up_proj, w_down, sources, item_count, model_width)


def on_device(tokens, norm_gain, expert_ids, gate_scores, w_gate, w_up, w_down):
    experts = lax.axis_size("ep")
    tok_rows, model_width = tokens.shape
    top_count = expert_ids.shape[1]
    capacity = 2 * tok_rows * top_count // experts
    floated = tokens.astype(jnp.float32)
    scaled = lax.rsqrt(jnp.mean(floated * floated, axis=1, keepdims=True) + 1e-06)
    normed = (floated * scaled * norm_gain[None, :]).astype(jnp.bfloat16)
    mixing = gate_scores / jnp.sum(gate_scores, axis=1, keepdims=True)
    flat_ids = expert_ids.reshape(-1)
    onehot = (flat_ids[:, None] == jnp.arange(experts, dtype=jnp.int32)[None, :]).astype(jnp.int32)
    before = jnp.cumsum(onehot, axis=0) - onehot
    slot_rank = jnp.sum(before * onehot, axis=1)
    positions = flat_ids * capacity + slot_rank
    token_slots = positions.reshape(tok_rows, top_count)
    buckets = jnp.arange(experts * capacity, dtype=jnp.int32)
    routing = jnp.any(token_slots[None, :, :] == buckets[:, None, None], axis=2).astype(
        jnp.bfloat16
    )
    outgoing = jnp.dot(routing, normed, preferred_element_type=jnp.float32).astype(jnp.bfloat16)
    outgoing = outgoing.reshape(experts, capacity, model_width)
    partial_value = expert_block(
        lax.all_to_all(outgoing, "ep", split_axis=0, concat_axis=0, tiled=True),
        w_gate,
        w_up,
        w_down,
    )
    summed = lax.psum_scatter(
        partial_value.astype(jnp.float32).astype(jnp.bfloat16),
        "grp",
        scatter_dimension=2,
        tiled=True,
    ).astype(jnp.float32)
    returned = lax.all_to_all(
        summed.astype(jnp.bfloat16), "ep", split_axis=0, concat_axis=0, tiled=True
    ).astype(summed.dtype)
    feature_count = returned.shape[2]
    picked = returned.reshape(experts * capacity, feature_count)[positions]
    picked = picked.reshape(tok_rows, top_count, feature_count)
    result = jnp.sum(picked * mixing[:, :, None], axis=1)
    return result.astype(jnp.bfloat16)


MESH = pl.DeviceIdType.MESH
LANES = 128
CHUNKS = 2


def tile_of(extent, most):
    tile = most
    while extent % tile:
        tile //= 2
    return tile


def ring_kernel(
    experts, x_ref, wg_ref, wu_ref, wd_ref, out_ref,
    rows_in, wg, wu, wd, hidden, pair_out, pair_in, own, cross_out, cross_in, ring_out, ring_in,
    gather_send, gather_recv, share_send, share_recv, pair_send, pair_recv,
    cross_send, cross_recv, ring_send, ring_recv, load_sem,
):
    slots, both, _ = rows_in.shape
    rows = both // 2
    units, width = wg.shape
    part = width // 2
    half = slots // 2
    me, grp = lax.axis_index("ep"), lax.axis_index("grp")
    chip, core = me // 2, me % 2
    column, level = chip % 2, chip // 2
    place = level + column * (slots - 1 - 2 * level)

    def at_place(p):
        col = p // half
        lev = p + col * (slots - 1 - 2 * p)
        return (lev * 2 + col) * 2 + core

    right = {"ep": at_place((place + 1) % slots)}
    left = {"ep": at_place((place + slots - 1) % slots)}
    partner = {"ep": chip * 2 + 1 - core}
    across = {"grp": 1 - grp}

    loads = [
        pltpu.make_async_copy(x_ref, rows_in.at[0, pl.ds(0, rows)], load_sem.at[0]),
        pltpu.make_async_copy(wg_ref.at[0], wg, load_sem.at[1]),
        pltpu.make_async_copy(wu_ref.at[0], wu, load_sem.at[2]),
        pltpu.make_async_copy(wd_ref.at[0], wd, load_sem.at[3]),
    ]
    for load in loads:
        load.start()

    barrier = pltpu.get_barrier_semaphore()
    for other in (left, right, partner, across):
        pl.semaphore_signal(barrier, inc=1, device_id=other, device_id_type=MESH)
    pl.semaphore_wait(barrier, 4)

    def remote(src, dst, send, recv, device):
        return pltpu.make_async_remote_copy(
            src_ref=src, dst_ref=dst, send_sem=send, recv_sem=recv, device_id=device, device_id_type=MESH
        )

    def slot_at(direction, distance):
        if distance == 0:
            return 0
        if distance == half:
            return slots - 1
        return 2 * distance - 1 + direction

    def block_slots(b):
        if b == 0:
            return 0, 1
        if b == half:
            return slots - 1, 1
        return 2 * b - 1, 2

    def gather_copy(direction, d):
        source, target = slot_at(direction, d - 1), slot_at(direction, d)
        span = pl.ds(0, rows)
        if d == half:
            span = pl.ds(direction * (rows // 2), rows // 2)
        return remote(
            rows_in.at[source, span], rows_in.at[target, span],
            gather_send.at[direction, d - 1], gather_recv.at[direction, d - 1],
            (right, left)[direction],
        )

    def share_copy(b):
        first, count = block_slots(b)
        return remote(
            rows_in.at[pl.ds(first, count), pl.ds(0, rows)], rows_in.at[pl.ds(first, count), pl.ds(rows, rows)],
            share_send.at[b], share_recv.at[b], partner,
        )

    def pair_copy(b):
        span = pl.ds(*block_slots(b))
        return remote(pair_out.at[span], pair_in.at[span], pair_send.at[b], pair_recv.at[b], partner)

    def cross_copy(b):
        span = pl.ds(*block_slots(b))
        return remote(cross_out.at[span], cross_in.at[span], cross_send.at[b], cross_recv.at[b], across)

    unit_tile = tile_of(units, 256)
    col_tile = tile_of(part, 512)

    def compute(b):
        first, count = block_slots(b)
        height = count * both
        slab = pl.ds(first, count)
        lanes = lax.broadcasted_iota(jnp.int32, (height, LANES), 1)
        shares = rows_in[slab, :, pl.ds(width, LANES)].astype(jnp.float32).reshape(height, LANES)
        weight = jnp.sum(
            jnp.where((lanes == me) | (lanes == me + experts), shares, 0.0), axis=1, keepdims=True
        )

        def up_step(j, carry):
            span = pl.ds(pl.multiple_of(j * unit_tile, unit_tile), unit_tile)
            block = rows_in[slab, :, pl.ds(0, width)].reshape(height, width)
            contract = (((1,), (1,)), ((), ()))
            gate = lax.dot_general(block, wg[span, :], contract, preferred_element_type=jnp.float32)
            upper = lax.dot_general(block, wu[span, :], contract, preferred_element_type=jnp.float32)
            value = gate / (1.0 + jnp.exp(-gate)) * upper * weight
            hidden[pl.ds(0, height), span] = value.astype(jnp.bfloat16)
            return carry

        lax.fori_loop(0, units // unit_tile, up_step, 0)
        if b == 0:
            loads[3].wait()

        for h in range(2):
            base = ((grp + 1 + h) % 2) * part

            def down_step(j, carry):
                held = pl.ds(pl.multiple_of(j * col_tile, col_tile), col_tile)
                span = pl.ds(pl.multiple_of(base + j * col_tile, col_tile), col_tile)
                value = jnp.dot(hidden[pl.ds(0, height), :], wd[:, span], preferred_element_type=jnp.float32)
                value = value.reshape(count, 2, rows, col_tile)
                own[h, slab, :, held] = value[:, 0]
                pair_out[slab, h, :, held] = value[:, 1].astype(jnp.bfloat16)
                return carry

            lax.fori_loop(0, part // col_tile, down_step, 0)
        pair_copy(b).start()

    def add_pair(b):
        first, count = block_slots(b)
        pair_copy(b).wait_recv()
        for s in range(first, first + count):
            cross_out[s] = (own[0, s] + pair_in[s, 0].astype(jnp.float32)).astype(jnp.bfloat16)
        cross_copy(b).start()
        for s in range(first, first + count):
            own[1, s] = own[1, s] + pair_in[s, 1].astype(jnp.float32)

    def add_cross(b):
        first, count = block_slots(b)
        cross_copy(b).wait_recv()
        for s in range(first, first + count):
            own[1, s] = own[1, s] + cross_in[s].astype(jnp.float32)

    loads[0].wait()
    for b in range(half + 1):
        if b > 0:
            for direction in range(2):
                gather_copy(direction, b).wait_recv()
        if b < half:
            for direction in range(2):
                gather_copy(direction, b + 1).start()
        share_copy(b).start()
        share_copy(b).wait_recv()
        if b == 0:
            loads[1].wait()
            loads[2].wait()
        compute(b)
        add_pair(b)
        if b > 0:
            add_cross(b - 1)
    add_cross(half)

    step_cols = part // CHUNKS

    def ring_copy(direction, t, c):
        span = pl.ds(0, rows)
        if t == 0:
            span = pl.ds(direction * (rows // 2), rows // 2)
        return remote(
            ring_out.at[direction, t, c, span], ring_in.at[direction, t, c, span],
            ring_send.at[direction, t, c], ring_recv.at[direction, t, c],
            (left, right)[direction],
        )

    for t in range(half):
        for c in range(CHUNKS):
            cols = pl.ds(c * step_cols, step_cols)
            for direction in range(2):
                slot = slot_at(direction, half - t)
                if t > 0:
                    ring_copy(direction, t - 1, c).wait_recv()
                for piece in range(2):
                    span = pl.ds(piece * (rows // 2), rows // 2)
                    if t == 0 and piece != direction:
                        continue
                    value = own[1, slot, span, cols]
                    if t > 1 or (t == 1 and piece == direction):
                        value = value + ring_in[direction, t - 1, c, span].astype(jnp.float32)
                    ring_out[direction, t, c, span] = value.astype(jnp.bfloat16)
                ring_copy(direction, t, c).start()
    for c in range(CHUNKS):
        cols = pl.ds(c * step_cols, step_cols)
        value = own[1, 0, :, cols]
        for direction in range(2):
            ring_copy(direction, half - 1, c).wait_recv()
            value = value + ring_in[direction, half - 1, c].astype(jnp.float32)
        out_ref[:, cols] = value.astype(out_ref.dtype)

    for b in range(half + 1):
        share_copy(b).wait_send()
        pair_copy(b).wait_send()
        cross_copy(b).wait_send()
    for direction in range(2):
        for d in range(half):
            gather_copy(direction, d + 1).wait_send()
            for c in range(CHUNKS):
                ring_copy(direction, d, c).wait_send()


def on_device_ring(tokens, norm_gain, expert_ids, gate_scores, w_gate, w_up, w_down):
    experts = lax.axis_size("ep")
    rows, width = tokens.shape
    units = w_gate.shape[1]
    slots = experts // 2
    half = slots // 2
    part = width // 2
    floated = tokens.astype(jnp.float32)
    scaled = lax.rsqrt(jnp.mean(floated * floated, axis=1, keepdims=True) + 1e-06)
    normed = (floated * scaled * norm_gain[None, :]).astype(jnp.bfloat16)
    mixing = gate_scores / jnp.sum(gate_scores, axis=1, keepdims=True)
    chosen = expert_ids[:, :, None] == jnp.arange(experts, dtype=jnp.int32)[None, None, :]
    dense = jnp.sum(jnp.where(chosen, mixing[:, :, None], 0.0), axis=1)
    upper = lax.reduce_precision(dense, 8, 7)
    shares = jnp.concatenate([upper, dense - upper], axis=1).astype(jnp.bfloat16)
    shares = jnp.pad(shares, ((0, 0), (0, LANES - 2 * experts)))
    packed = jnp.concatenate([normed, shares], axis=1)
    dma = pltpu.SemaphoreType.DMA
    bf16, f32 = jnp.bfloat16, jnp.float32
    return pl.pallas_call(
        functools.partial(ring_kernel, experts),
        out_shape=jax.ShapeDtypeStruct((rows, part), bf16),
        in_specs=[pl.BlockSpec(memory_space=pl.ANY)] * 4,
        out_specs=pl.BlockSpec(memory_space=pltpu.VMEM),
        scratch_shapes=[
            pltpu.VMEM((slots, 2 * rows, width + LANES), bf16),
            pltpu.VMEM((units, width), bf16),
            pltpu.VMEM((units, width), bf16),
            pltpu.VMEM((units, width), bf16),
            pltpu.VMEM((4 * rows, units), bf16),
            pltpu.VMEM((slots, 2, rows, part), bf16),
            pltpu.VMEM((slots, 2, rows, part), bf16),
            pltpu.VMEM((2, slots, rows, part), f32),
            pltpu.VMEM((slots, rows, part), bf16),
            pltpu.VMEM((slots, rows, part), bf16),
            pltpu.VMEM((2, half, CHUNKS, rows, part // CHUNKS), bf16),
            pltpu.VMEM((2, half, CHUNKS, rows, part // CHUNKS), bf16),
            dma((2, half)), dma((2, half)),
            dma((half + 1,)), dma((half + 1,)),
            dma((half + 1,)), dma((half + 1,)),
            dma((half + 1,)), dma((half + 1,)),
            dma((2, half, CHUNKS)), dma((2, half, CHUNKS)),
            dma((4,)),
        ],
        compiler_params=pltpu.CompilerParams(
            collective_id=0, has_side_effects=True, vmem_limit_bytes=62 * 1024 * 1024
        ),
    )(packed, w_gate, w_up, w_down)


def solution(mesh):
    groups, experts = mesh.shape["grp"], mesh.shape["ep"]

    def body(tokens, norm_gain, expert_ids, gate_scores, w_gate, w_up, w_down):
        capacity = 2 * tokens.shape[0] * expert_ids.shape[1] // experts
        whole_slabs = capacity >= tokens.shape[0] and w_gate.shape[0] == 1
        ringable = groups == 2 and experts % 4 == 0 and experts >= 8 and 2 * experts <= LANES
        chosen = on_device_ring if whole_slabs and ringable else on_device
        return chosen(tokens, norm_gain, expert_ids, gate_scores, w_gate, w_up, w_down)

    return jax.shard_map(
        body,
        mesh=mesh,
        in_specs=(
            P("ep", None),
            P(),
            P("ep", None),
            P("ep", None),
            P("ep", "grp", None),
            P("ep", "grp", None),
            P("ep", "grp", None),
        ),
        out_specs=P("ep", "grp"),
        check_vma=False,
    )
```

```python
import functools

import jax
import jax.numpy as jnp
from jax import lax
from jax.experimental import pallas as pl
from jax.experimental.pallas import tpu as pltpu
from jax.sharding import PartitionSpec as P


def finish_expert(gate_proj, up_proj, w_down, sources, item_count, model_width):
    hidden = (jax.nn.silu(gate_proj) * up_proj).astype(jnp.bfloat16)
    outputs = jnp.dot(hidden, w_down[0], preferred_element_type=jnp.float32).astype(jnp.bfloat16)
    return outputs.reshape(sources, item_count, model_width)


def expert_block(received, w_gate, w_up, w_down):
    sources, item_count, model_width = received.shape
    flat_rows = received.reshape(sources * item_count, model_width)
    contract = (((1,), (1,)), ((), ()))
    gate_proj = lax.dot_general(flat_rows, w_gate[0], contract, preferred_element_type=jnp.float32)
    up_proj = lax.dot_general(flat_rows, w_up[0], contract, preferred_element_type=jnp.float32)
    return finish_expert(gate_proj, up_proj, w_down, sources, item_count, model_width)


def on_device(tokens, norm_gain, expert_ids, gate_scores, w_gate, w_up, w_down):
    experts = lax.axis_size("ep")
    tok_rows, model_width = tokens.shape
    top_count = expert_ids.shape[1]
    capacity = 2 * tok_rows * top_count // experts
    floated = tokens.astype(jnp.float32)
    scaled = lax.rsqrt(jnp.mean(floated * floated, axis=1, keepdims=True) + 1e-06)
    normed = (floated * scaled * norm_gain[None, :]).astype(jnp.bfloat16)
    mixing = gate_scores / jnp.sum(gate_scores, axis=1, keepdims=True)
    flat_ids = expert_ids.reshape(-1)
    onehot = (flat_ids[:, None] == jnp.arange(experts, dtype=jnp.int32)[None, :]).astype(jnp.int32)
    before = jnp.cumsum(onehot, axis=0) - onehot
    slot_rank = jnp.sum(before * onehot, axis=1)
    positions = flat_ids * capacity + slot_rank
    token_slots = positions.reshape(tok_rows, top_count)
    buckets = jnp.arange(experts * capacity, dtype=jnp.int32)
    routing = jnp.any(token_slots[None, :, :] == buckets[:, None, None], axis=2).astype(
        jnp.bfloat16
    )
    outgoing = jnp.dot(routing, normed, preferred_element_type=jnp.float32).astype(jnp.bfloat16)
    outgoing = outgoing.reshape(experts, capacity, model_width)
    partial_value = expert_block(
        lax.all_to_all(outgoing, "ep", split_axis=0, concat_axis=0, tiled=True),
        w_gate,
        w_up,
        w_down,
    )
    summed = lax.psum_scatter(
        partial_value.astype(jnp.float32).astype(jnp.bfloat16),
        "grp",
        scatter_dimension=2,
        tiled=True,
    ).astype(jnp.float32)
    returned = lax.all_to_all(
        summed.astype(jnp.bfloat16), "ep", split_axis=0, concat_axis=0, tiled=True
    ).astype(summed.dtype)
    feature_count = returned.shape[2]
    picked = returned.reshape(experts * capacity, feature_count)[positions]
    picked = picked.reshape(tok_rows, top_count, feature_count)
    result = jnp.sum(picked * mixing[:, :, None], axis=1)
    return result.astype(jnp.bfloat16)


MESH = pl.DeviceIdType.MESH
LANES = 128
CHUNKS = 2
EARLY_SHARE = 4


def tile_of(extent, most):
    tile = most
    while extent % tile:
        tile //= 2
    return tile


def ring_kernel(
    experts, tokens_ref, gain_ref, ids_ref, scores_ref, wg_ref, wu_ref, wd_ref, out_ref,
    rows_in, wg, wu, wd, hidden, pair_out, pair_in, own, cross_out, cross_in, ring_out, ring_in,
    first_out, first_in, last_out, last_in,
    gather_send, gather_recv, share_send, share_recv, pair_send, pair_recv,
    cross_send, cross_recv, ring_send, ring_recv, first_send, first_recv, last_sem, load_sem,
):
    slots, both, _ = rows_in.shape
    rows = both // 2
    units, width = wg.shape
    part = width // 2
    half = slots // 2
    early = first_out.shape[-1]
    late = part - early
    me, grp = lax.axis_index("ep"), lax.axis_index("grp")
    chip, core = me // 2, me % 2
    column, level = chip % 2, chip // 2
    place = level + column * (slots - 1 - 2 * level)

    def at_place(p):
        col = p // half
        lev = p + col * (slots - 1 - 2 * p)
        return (lev * 2 + col) * 2 + core

    right = {"ep": at_place((place + 1) % slots)}
    left = {"ep": at_place((place + slots - 1) % slots)}
    partner = {"ep": chip * 2 + 1 - core}
    across = {"grp": 1 - grp}

    loads = [
        pltpu.make_async_copy(wg_ref.at[0], wg, load_sem.at[0]),
        pltpu.make_async_copy(wu_ref.at[0], wu, load_sem.at[1]),
        pltpu.make_async_copy(wd_ref.at[0], wd, load_sem.at[2]),
    ]
    for load in loads:
        load.start()

    barrier = pltpu.get_barrier_semaphore()
    for other in (left, right, partner, across):
        pl.semaphore_signal(barrier, inc=1, device_id=other, device_id_type=MESH)

    row_tile = tile_of(rows, 16)

    def normalise(r, carry):
        span = pl.ds(pl.multiple_of(r * row_tile, row_tile), row_tile)
        floated = tokens_ref[span, :].astype(jnp.float32)
        scaled = lax.rsqrt(jnp.mean(floated * floated, axis=1, keepdims=True) + 1e-06)
        rows_in[0, span, pl.ds(0, width)] = (floated * scaled * gain_ref[...]).astype(jnp.bfloat16)
        scores = scores_ref[span, :]
        mixing = scores / jnp.sum(scores, axis=1, keepdims=True)
        ids = ids_ref[span, :]
        lanes = lax.broadcasted_iota(jnp.int32, (row_tile, LANES), 1)
        upper = jnp.zeros((row_tile, LANES), jnp.float32)
        lower = jnp.zeros((row_tile, LANES), jnp.float32)
        for k in range(ids.shape[1]):
            upper = jnp.where(lanes == ids[:, k:k + 1], mixing[:, k:k + 1], upper)
            lower = jnp.where(lanes == ids[:, k:k + 1] + experts, mixing[:, k:k + 1], lower)
        lower = lower - lower.astype(jnp.bfloat16).astype(jnp.float32)
        rows_in[0, span, pl.ds(width, LANES)] = jnp.where(lanes < experts, upper, lower).astype(jnp.bfloat16)
        return carry

    lax.fori_loop(0, rows // row_tile, normalise, 0)
    pl.semaphore_wait(barrier, 4)

    def remote(src, dst, send, recv, device):
        return pltpu.make_async_remote_copy(
            src_ref=src, dst_ref=dst, send_sem=send, recv_sem=recv, device_id=device, device_id_type=MESH
        )

    def slot_at(direction, distance):
        if distance == 0:
            return 0
        if distance == half:
            return slots - 1
        return 2 * distance - 1 + direction

    def block_slots(b):
        if b == 0:
            return 0, 1
        if b == half:
            return slots - 1, 1
        return 2 * b - 1, 2

    def gather_rows(direction, d, piece):
        if d == half:
            return direction * (rows // 2) + piece * (rows // 4), rows // 4
        return (piece ^ direction) * (rows // 2), rows // 2

    def gather_copy(direction, d, piece):
        source, target = slot_at(direction, d - 1), slot_at(direction, d)
        span = pl.ds(*gather_rows(direction, d, piece))
        return remote(
            rows_in.at[source, span], rows_in.at[target, span],
            gather_send.at[direction, d - 1, piece], gather_recv.at[direction, d - 1, piece],
            (right, left)[direction],
        )

    def share_copy(direction, d, piece):
        slot = slot_at(direction, d)
        start, count = gather_rows(direction, d, piece)
        return remote(
            rows_in.at[slot, pl.ds(start, count)], rows_in.at[slot, pl.ds(rows + start, count)],
            share_send.at[direction, d, piece], share_recv.at[direction, d, piece], partner,
        )

    def share_list(d):
        if d == 0:
            return [share_copy(0, 0, 0), share_copy(0, 0, 1)]
        return [share_copy(direction, d, piece) for piece in range(2) for direction in range(2)]

    def forward(d, piece):
        for direction in range(2):
            gather_copy(direction, d, piece).wait_recv()
            if d + 1 < half:
                gather_copy(direction, d + 1, piece).start()
            elif d + 1 == half and piece == 0:
                gather_copy(direction, half, 0).start()
                gather_copy(direction, half, 1).start()
            share_copy(direction, d, piece).start()

    def pair_copy(b):
        span = pl.ds(*block_slots(b))
        return remote(pair_out.at[span], pair_in.at[span], pair_send.at[b], pair_recv.at[b], partner)

    def cross_copy(b):
        span = pl.ds(*block_slots(b))
        return remote(cross_out.at[span], cross_in.at[span], cross_send.at[b], cross_recv.at[b], across)

    unit_tile = tile_of(units, 256)
    col_tile = tile_of(part, 512)

    def compute(b):
        first, count = block_slots(b)
        height = count * both
        slab = pl.ds(first, count)
        lanes = lax.broadcasted_iota(jnp.int32, (height, LANES), 1)
        shares = rows_in[slab, :, pl.ds(width, LANES)].astype(jnp.float32).reshape(height, LANES)
        weight = jnp.sum(
            jnp.where((lanes == me) | (lanes == me + experts), shares, 0.0), axis=1, keepdims=True
        )

        def up_step(j, carry):
            span = pl.ds(pl.multiple_of(j * unit_tile, unit_tile), unit_tile)
            block = rows_in[slab, :, pl.ds(0, width)].reshape(height, width)
            contract = (((1,), (1,)), ((), ()))
            gate = lax.dot_general(block, wg[span, :], contract, preferred_element_type=jnp.float32)
            upper = lax.dot_general(block, wu[span, :], contract, preferred_element_type=jnp.float32)
            value = gate / (1.0 + jnp.exp(-gate)) * upper * weight
            hidden[pl.ds(0, height), span] = value.astype(jnp.bfloat16)
            return carry

        lax.fori_loop(0, units // unit_tile, up_step, 0)
        if b < half:
            forward(b + 1, 0)
        if b == 0:
            loads[2].wait()

        for h in range(2):
            base = ((grp + 1 + h) % 2) * part

            def down_step(j, carry):
                held = pl.ds(pl.multiple_of(j * col_tile, col_tile), col_tile)
                span = pl.ds(pl.multiple_of(base + j * col_tile, col_tile), col_tile)
                value = jnp.dot(hidden[pl.ds(0, height), :], wd[:, span], preferred_element_type=jnp.float32)
                value = value.reshape(count, 2, rows, col_tile)
                own[h, slab, :, held] = value[:, 0]
                pair_out[slab, h, :, held] = value[:, 1].astype(jnp.bfloat16)
                return carry

            lax.fori_loop(0, part // col_tile, down_step, 0)
        pair_copy(b).start()

    def add_pair(b):
        first, count = block_slots(b)
        pair_copy(b).wait_recv()
        for s in range(first, first + count):
            total = own[0, s, :, pl.ds(early, late)] + pair_in[s, 0, :, pl.ds(early, late)].astype(jnp.float32)
            cross_out[s] = total.astype(jnp.bfloat16)
        cross_copy(b).start()
        for s in range(first, first + count):
            own[0, s, :, pl.ds(0, early)] += pair_in[s, 0, :, pl.ds(0, early)].astype(jnp.float32)
            own[1, s] += pair_in[s, 1].astype(jnp.float32)

    def add_cross(b):
        first, count = block_slots(b)
        cross_copy(b).wait_recv()
        for s in range(first, first + count):
            own[1, s, :, pl.ds(early, late)] += cross_in[s].astype(jnp.float32)

    for piece in range(2):
        for direction in range(2):
            gather_copy(direction, 1, piece).start()
    for copy in share_list(0):
        copy.start()
    for b in range(half + 1):
        if b > 0:
            forward(b, 1)
        for copy in share_list(b):
            copy.wait_recv()
        if b == 0:
            loads[0].wait()
            loads[1].wait()
        compute(b)
        add_pair(b)
        if b > 1:
            add_cross(b - 2)

    step_cols = late // CHUNKS

    def ring_rows(direction, t):
        return pl.ds(direction * (rows // 2), rows // 2) if t == 0 else pl.ds(0, rows)

    def ring_copy(direction, t, c):
        span = ring_rows(direction, t)
        return remote(
            ring_out.at[direction, t, c, span], ring_in.at[direction, t, c, span],
            ring_send.at[direction, t, c], ring_recv.at[direction, t, c],
            (left, right)[direction],
        )

    def first_copy(direction, t):
        span = ring_rows(direction, t)
        return remote(
            first_out.at[direction, t, :, span], first_in.at[direction, t, :, span],
            first_send.at[direction, t], first_recv.at[direction, t],
            (left, right)[direction],
        )

    def last_copy():
        return remote(last_out, last_in, last_sem.at[0], last_sem.at[1], across)

    def first_step(t):
        for direction in range(2):
            slot = slot_at(direction, half - t)
            if t > 0:
                first_copy(direction, t - 1).wait_recv()
            for piece in range(2):
                span = pl.ds(piece * (rows // 2), rows // 2)
                if t == 0 and piece != direction:
                    continue
                value = own[:, slot, span, pl.ds(0, early)]
                if t > 1 or (t == 1 and piece == direction):
                    value = value + first_in[direction, t - 1, :, span].astype(jnp.float32)
                first_out[direction, t, :, span] = value.astype(jnp.bfloat16)
            first_copy(direction, t).start()

    def ring_step(t):
        for c in range(CHUNKS):
            cols = pl.ds(early + c * step_cols, step_cols)
            for direction in range(2):
                slot = slot_at(direction, half - t)
                if t > 0:
                    ring_copy(direction, t - 1, c).wait_recv()
                for piece in range(2):
                    span = pl.ds(piece * (rows // 2), rows // 2)
                    if t == 0 and piece != direction:
                        continue
                    value = own[1, slot, span, cols]
                    if t > 1 or (t == 1 and piece == direction):
                        value = value + ring_in[direction, t - 1, c, span].astype(jnp.float32)
                    ring_out[direction, t, c, span] = value.astype(jnp.bfloat16)
                ring_copy(direction, t, c).start()

    first_step(0)
    add_cross(half - 1)
    first_step(1)
    add_cross(half)
    for t in range(half):
        ring_step(t)
        if t + 2 < half:
            first_step(t + 2)
        elif t + 2 == half:
            totals = own[:, 0, :, pl.ds(0, early)]
            for direction in range(2):
                first_copy(direction, half - 1).wait_recv()
                totals = totals + first_in[direction, half - 1].astype(jnp.float32)
            last_out[...] = totals[0].astype(jnp.bfloat16)
            last_copy().start()
            own[1, 0, :, pl.ds(0, early)] = totals[1]
    last_copy().wait_recv()
    head = own[1, 0, :, pl.ds(0, early)] + last_in[...].astype(jnp.float32)
    out_ref[:, pl.ds(0, early)] = head.astype(out_ref.dtype)
    for c in range(CHUNKS):
        cols = pl.ds(early + c * step_cols, step_cols)
        value = own[1, 0, :, cols]
        for direction in range(2):
            ring_copy(direction, half - 1, c).wait_recv()
            value = value + ring_in[direction, half - 1, c].astype(jnp.float32)
        out_ref[:, cols] = value.astype(out_ref.dtype)

    last_copy().wait_send()
    for b in range(half + 1):
        for copy in share_list(b):
            copy.wait_send()
        pair_copy(b).wait_send()
        cross_copy(b).wait_send()
    for direction in range(2):
        for d in range(half):
            first_copy(direction, d).wait_send()
            for piece in range(2):
                gather_copy(direction, d + 1, piece).wait_send()
            for c in range(CHUNKS):
                ring_copy(direction, d, c).wait_send()


def on_device_ring(tokens, norm_gain, expert_ids, gate_scores, w_gate, w_up, w_down):
    experts = lax.axis_size("ep")
    rows, width = tokens.shape
    units = w_gate.shape[1]
    slots = experts // 2
    half = slots // 2
    part = width // 2
    early = part // EARLY_SHARE
    late = part - early
    dma = pltpu.SemaphoreType.DMA
    bf16, f32 = jnp.bfloat16, jnp.float32
    return pl.pallas_call(
        functools.partial(ring_kernel, experts),
        out_shape=jax.ShapeDtypeStruct((rows, part), bf16),
        in_specs=[pl.BlockSpec(memory_space=pltpu.VMEM)] * 4 + [pl.BlockSpec(memory_space=pl.ANY)] * 3,
        out_specs=pl.BlockSpec(memory_space=pltpu.VMEM),
        scratch_shapes=[
            pltpu.VMEM((slots, 2 * rows, width + LANES), bf16),
            pltpu.VMEM((units, width), bf16),
            pltpu.VMEM((units, width), bf16),
            pltpu.VMEM((units, width), bf16),
            pltpu.VMEM((4 * rows, units), bf16),
            pltpu.VMEM((slots, 2, rows, part), bf16),
            pltpu.VMEM((slots, 2, rows, part), bf16),
            pltpu.VMEM((2, slots, rows, part), f32),
            pltpu.VMEM((slots, rows, late), bf16),
            pltpu.VMEM((slots, rows, late), bf16),
            pltpu.VMEM((2, half, CHUNKS, rows, late // CHUNKS), bf16),
            pltpu.VMEM((2, half, CHUNKS, rows, late // CHUNKS), bf16),
            pltpu.VMEM((2, half, 2, rows, early), bf16),
            pltpu.VMEM((2, half, 2, rows, early), bf16),
            pltpu.VMEM((rows, early), bf16),
            pltpu.VMEM((rows, early), bf16),
            dma((2, half, 2)), dma((2, half, 2)),
            dma((2, half + 1, 2)), dma((2, half + 1, 2)),
            dma((half + 1,)), dma((half + 1,)),
            dma((half + 1,)), dma((half + 1,)),
            dma((2, half, CHUNKS)), dma((2, half, CHUNKS)),
            dma((2, half)), dma((2, half)), dma((2,)),
            dma((3,)),
        ],
        compiler_params=pltpu.CompilerParams(
            collective_id=0, has_side_effects=True, vmem_limit_bytes=62 * 1024 * 1024
        ),
    )(tokens, norm_gain[None, :], expert_ids, gate_scores, w_gate, w_up, w_down)


def solution(mesh):
    groups, experts = mesh.shape["grp"], mesh.shape["ep"]

    def body(tokens, norm_gain, expert_ids, gate_scores, w_gate, w_up, w_down):
        capacity = 2 * tokens.shape[0] * expert_ids.shape[1] // experts
        whole_slabs = capacity >= tokens.shape[0] and w_gate.shape[0] == 1
        ringable = groups == 2 and experts % 4 == 0 and experts >= 8 and 2 * experts <= LANES
        chosen = on_device_ring if whole_slabs and ringable else on_device
        return chosen(tokens, norm_gain, expert_ids, gate_scores, w_gate, w_up, w_down)

    return jax.shard_map(
        body,
        mesh=mesh,
        in_specs=(
            P("ep", None),
            P(),
            P("ep", None),
            P("ep", None),
            P("ep", "grp", None),
            P("ep", "grp", None),
            P("ep", "grp", None),
        ),
        out_specs=P("ep", "grp"),
        check_vma=False,
    )
```
